512 devices in a mesh: day: 32 (over z, y_hi), sta: 16 (over y_lo, x, core).
Axes of the slice: x: 4, y: 8 (y_hi: 4, y_lo: 2; y = y_hi * 2 + y_lo), z: 8, core: 2. Of those that a mesh axis runs over, the one named last changes fastest.
Arguments:
- spectra: bfloat16 [2048, 2, 3, 384, 128], P('day', None, None, 'sta'), may hold values from -6 to 6
- src_block: int32 [2], replicated, may hold values from 0 to 15, as said below
- group_of: int32 [2048], replicated, may hold values from 0 to 1, as said below
- owner: int32 [32], replicated, may hold values from 0 to 31, each once
Outputs:
- owned_stacks: float32 [32, 96, 2, 9, 128], P('day', 'sta')
The draws below stay inside these ranges and needn't reach their ends.
Inputs may be any that keep to these rules, and one draw needn't show every extreme that they name: `src_block`: the two entries differ. `group_of`: every one of the 2 groups has at least one segment. `owner`: each day index owns exactly one pair block.
All inputs are finite; a program needn't handle non-finite values.
Results may differ from the reference program's by a relative error of at most 0.0003.
Values may be sent and summed in bfloat16 or wider, within the bound.
A program may use at most 64 MiB of HBM per device.

```python
import jax
import jax.numpy as jnp
from jax import lax

F = 128
LAG = 128
G = 2
SB = 4
R = 24
S = 8
STATIONS = 384
SEGS = 2048
PB = 6
PAIRS = 96
N_DAY = 32
N_STA = 16


def draw_src_block(key, part):
    blocks = STATIONS // R
    other = jax.random.randint(jax.random.fold_in(key, 11), (), 0, blocks - 1)
    flipped = jax.random.randint(jax.random.fold_in(key, 12), (), 0, 2)
    last = jnp.int32(blocks - 1)
    first_entry = jnp.where(flipped == 1, other, last)
    second_entry = jnp.where(flipped == 1, last, other)
    return jnp.stack([first_entry, second_entry]).astype(jnp.int32)


def draw_group_of(key, part):
    drawn = jax.random.randint(jax.random.fold_in(key, 21), (SEGS,), 0, G)
    positions = jnp.arange(SEGS, dtype=jnp.int32)
    return jnp.where(positions < G, positions, drawn).astype(jnp.int32)


def levels(stream_key, extent, cuts, low, largest):
    def one(axis_at, parts):
        steps = jax.random.uniform(jax.random.fold_in(jax.random.fold_in(stream_key, 6), axis_at), (parts,), jnp.float32, low / len(cuts), largest / len(cuts))
        return jnp.repeat(jnp.exp(steps), extent[axis_at] // parts).reshape((-1,) + (1,) * (len(extent) - axis_at - 1))

    gain = one(*cuts[0])
    for cut in cuts[1:]:
        gain = gain * one(*cut)
    return gain


def centred(rng, dims, deviation, bound, split=(), kind=jnp.bfloat16):
    gain = levels(rng, dims, split, -0.22, 0.18) if split else 1.0
    values = jax.random.normal(rng, dims, jnp.float32) * deviation * gain
    return jnp.minimum(jnp.maximum(values, -bound), bound).astype(kind)


def setup_inputs(seed: int = 0) -> dict:
    key_list = jax.random.split(jax.random.key(seed), 5)
    return {
        "spectra": centred(key_list[0], (SEGS, 2, 3, STATIONS, F), 1.0, 6.0, ((0, 32), (3, 16))),
        "src_block": draw_src_block(jax.random.fold_in(key_list[4], 71), 0),
        "group_of": draw_group_of(jax.random.fold_in(key_list[4], 71), 0),
        "owner": jax.random.permutation(key_list[3], N_DAY).astype(jnp.int32),
    }


def lag_table(freqs, lags):
    freq_ids = jnp.arange(freqs, dtype=jnp.int32)
    lag_ids = jnp.arange(lags, dtype=jnp.int32) - lags // 2
    phase = jnp.mod(freq_ids[:, None] * lag_ids[None, :], 2 * freqs)
    angle = 2.0 * jnp.pi / (2 * freqs) * phase.astype(jnp.float32)
    weight = jnp.where(freq_ids == 0, 1.0, 2.0).astype(jnp.float32) / jnp.sqrt(jnp.float32(freqs))
    return jnp.concatenate([weight[:, None] * jnp.cos(angle), -weight[:, None] * jnp.sin(angle)], axis=0)

def reference(spectra, src_block, group_of, owner):
    station_ids = (src_block[:, None] * R + jnp.arange(SB, dtype=jnp.int32)[None, :]).reshape(-1).astype(jnp.int32)
    source_values = jnp.take(spectra, station_ids, axis=3).astype(jnp.float32)
    receiver_values = spectra.astype(jnp.float32)
    onehot = (group_of[None, :] == jnp.arange(G, dtype=jnp.int32)[:, None]).astype(jnp.float32)
    counts = lax.optimization_barrier(jnp.sum(onehot, axis=1))
    weighted = onehot[:, :, None, None, None, None] * source_values[None]
    real_part = jnp.einsum('gtpasf,tpbrf->srgabf', weighted, receiver_values)
    swapped = jnp.stack([receiver_values[:, 1], -receiver_values[:, 0]], axis=1)
    imag_part = jnp.einsum('gtpasf,tpbrf->srgabf', weighted, swapped)
    scale_rows = 1.0 / jnp.sqrt(counts)
    spectra_pairs = jnp.concatenate([real_part, imag_part], axis=-1) * scale_rows[None, None, :, None, None, None]
    table = lag_table(F, LAG)
    lagged = jnp.dot(spectra_pairs.reshape(-1, 2 * F), table, precision=lax.Precision.HIGHEST)
    lagged = lagged.reshape(S, N_STA, R, G, 9, LAG).transpose(1, 0, 2, 3, 4, 5)
    lagged = lagged.reshape(N_STA, N_DAY, PB, G, 9, LAG)
    day_ids = jnp.arange(N_DAY, dtype=jnp.int32)
    inverse = lax.optimization_barrier(jnp.sum(day_ids[None, :] * (owner[None, :] == day_ids[:, None]).astype(jnp.int32), axis=1)).astype(jnp.int32)
    ordered = jnp.take(lagged, inverse, axis=1).transpose(1, 0, 2, 3, 4, 5)
    return ordered.reshape(N_DAY, PAIRS, G, 9, LAG)
```

```python
import jax
import jax.numpy as jnp
import numpy as np
from jax import lax
from jax.experimental import pallas as pl
from jax.experimental.pallas import tpu as pltpu
from jax.sharding import PartitionSpec as P

F = 128
LAG = 128
G = 2
SB = 4
S = 8
PB = 6
SEG = 64
R = 24
N_STA = 16
N_DAY = 32
N_Z = 8
N_Y = 4
PIECE = SEG // N_STA
ROWS = 112
UNROLL = 4
MESH = pl.DeviceIdType.MESH
VMEM_LIMIT = 48 * 1024 * 1024


def lag_tables():
    freq = np.arange(F)
    lag = np.arange(LAG) - LAG // 2
    angle = 2.0 * np.pi / (2 * F) * np.mod(freq[:, None] * lag[None, :], 2 * F)
    weight = np.where(freq == 0, 1.0, 2.0) / np.sqrt(F)
    table = np.concatenate(
        [weight[:, None] * np.cos(angle), -weight[:, None] * np.sin(angle)], axis=0
    )
    high = table.astype(jnp.bfloat16)
    low = (table - high.astype(np.float64)).astype(jnp.bfloat16)
    return high, low


def share_kernel(
    src_ref, spec_ref, out_ref, tiles, mine, seen, in_sem, a_send, a_recv, b_send, b_recv, c_send, c_recv
):
    me = lax.axis_index("sta")
    partner = me + 1 - 2 * lax.rem(me, 2)
    fetch = pltpu.make_async_copy(spec_ref.at[:, :, :, :, pl.ds(0, 8), :], tiles, in_sem)
    fetch.start()
    barrier = pltpu.get_barrier_semaphore()
    for step in range(1, N_STA):
        pl.semaphore_signal(
            barrier, inc=1, device_id={"sta": lax.rem(me + step, N_STA)}, device_id_type=MESH
        )
    pl.semaphore_wait(barrier, N_STA - 1)
    fetch.wait()
    for part in range(2):
        for comp in range(3):
            row = (part * 3 + comp) * SB
            mine[:, :, row : row + SB, :] = tiles[:, :, part, comp, 0:SB, :]

    def scatter(step):
        to = lax.rem(me + step, N_STA)
        return pltpu.make_async_remote_copy(
            src_ref=mine.at[to],
            dst_ref=seen.at[me],
            send_sem=a_send.at[step - 1],
            recv_sem=a_recv.at[step - 1],
            device_id={"sta": to},
            device_id_type=MESH,
        )

    scatters = [scatter(step) for step in range(1, N_STA)]
    for copy in scatters:
        copy.start()
    seen[me] = mine[me]
    for copy in scatters:
        copy.wait_recv()
    for block in range(2):
        out_ref[me, block] = seen[src_ref[block]]

    def spread(step):
        to = lax.rem(me + 2 * step, N_STA)
        return pltpu.make_async_remote_copy(
            src_ref=out_ref.at[me],
            dst_ref=out_ref.at[me],
            send_sem=b_send.at[step - 1],
            recv_sem=b_recv.at[step - 1],
            device_id={"sta": to},
            device_id_type=MESH,
        )

    def hand_over(step):
        piece = lax.rem(me + N_STA - 2 * step, N_STA)
        return pltpu.make_async_remote_copy(
            src_ref=out_ref.at[piece],
            dst_ref=out_ref.at[piece],
            send_sem=c_send.at[step],
            recv_sem=c_recv.at[step],
            device_id={"sta": partner},
            device_id_type=MESH,
        )

    half = N_STA // 2
    spreads = [spread(step) for step in range(1, half)]
    hands = [hand_over(step) for step in range(half)]
    for copy in spreads:
        copy.start()
    hands[0].start()
    for step in range(1, half):
        spreads[step - 1].wait_recv()
        hands[step].start()
    for copy in hands:
        copy.wait_recv()
    for copy in scatters + spreads + hands:
        copy.wait_send()


def share(src_block, spectra):
    pieces = spectra.reshape(N_STA, PIECE, 2, 3, R, F)
    half = N_STA // 2
    return pl.pallas_call(
        share_kernel,
        out_shape=jax.ShapeDtypeStruct((N_STA, 2, PIECE, 6 * SB, F), jnp.bfloat16),
        in_specs=[
            pl.BlockSpec(memory_space=pltpu.SMEM),
            pl.BlockSpec(memory_space=pl.ANY),
        ],
        out_specs=pl.BlockSpec(memory_space=pltpu.VMEM),
        scratch_shapes=[
            pltpu.VMEM((N_STA, PIECE, 2, 3, 8, F), jnp.bfloat16),
            pltpu.VMEM((N_STA, PIECE, 6 * SB, F), jnp.bfloat16),
            pltpu.VMEM((N_STA, PIECE, 6 * SB, F), jnp.bfloat16),
            pltpu.SemaphoreType.DMA,
            pltpu.SemaphoreType.DMA((N_STA - 1,)),
            pltpu.SemaphoreType.DMA((N_STA - 1,)),
            pltpu.SemaphoreType.DMA((half - 1,)),
            pltpu.SemaphoreType.DMA((half - 1,)),
            pltpu.SemaphoreType.DMA((half,)),
            pltpu.SemaphoreType.DMA((half,)),
        ],
        compiler_params=pltpu.CompilerParams(
            collective_id=0, has_side_effects=True, vmem_limit_bytes=VMEM_LIMIT
        ),
        name="share",
    )(src_block, pieces)


def stack_kernel(
    day_ref, group_ref, owner_ref, group_tile_ref, spec_ref, source_ref, high_ref, low_ref,
    out_ref, rec_re, rec_im, rec_sum, src_re, src_im, src_dif, cross, lagged, order,
):
    first = day_ref[0] * SEG

    def clear(i, carry):
        order[0, i] = SEG
        order[1, i] = SEG
        return carry

    lax.fori_loop(0, SEG + UNROLL, clear, 0)

    def sort(t, carry):
        zeros, ones = carry
        group = group_ref[first + t]
        order[group, jnp.where(group == 0, zeros, ones)] = t
        return zeros + 1 - group, ones + group

    zeros, ones = lax.fori_loop(0, SEG, sort, (jnp.int32(0), jnp.int32(0)))

    def widen(t, carry):
        for comp in range(3):
            real = spec_ref[t, 0, comp].astype(jnp.float32)
            imag = spec_ref[t, 1, comp].astype(jnp.float32)
            rec_re[t, comp] = real
            rec_im[t, comp] = imag
            rec_sum[t, comp] = real + imag
        for block in range(2):
            rows = source_ref[t // PIECE, block, lax.rem(t, PIECE)].astype(jnp.float32)
            real, imag = rows[: 3 * SB], rows[3 * SB :]
            at = pl.ds(block * 3 * SB, 3 * SB)
            src_re[t, at] = real
            src_im[t, at] = imag
            src_dif[t, at] = real - imag
        return carry

    lax.fori_loop(0, SEG, widen, 0)
    blank = jnp.zeros((6 * SB, F), jnp.float32)
    src_re[SEG] = blank
    src_im[SEG] = blank
    src_dif[SEG] = blank

    def one_source(s, carry):
        base = (s // SB) * 3 * SB + lax.rem(s, SB)
        for group in range(G):
            steps = (zeros if group == 0 else ones) + UNROLL - 1
            for tile in range(3):

                def walk(step, sums):
                    sums = list(sums)
                    for turn in range(UNROLL):
                        t = order[group, step * UNROLL + turn]
                        at = jnp.minimum(t, SEG - 1)
                        rec = []
                        for comp in range(3):
                            place = pl.ds(tile * 8, 8)
                            rec.append(
                                (rec_re[at, comp, place], rec_im[at, comp, place], rec_sum[at, comp, place])
                            )
                        for a in range(3):
                            row = pl.ds(base + a * SB, 8, stride=0)
                            src = (src_re[t, row], src_im[t, row], src_dif[t, row])
                            for b in range(3):
                                for k in range(3):
                                    i = (a * 3 + b) * 3 + k
                                    sums[i] = sums[i] + src[k] * rec[b][k]
                    return tuple(sums)

                zero = jnp.zeros((8, F), jnp.float32)
                sums = lax.fori_loop(0, steps // UNROLL, walk, (zero,) * 27)
                for c in range(9):
                    one, two, three = sums[3 * c : 3 * c + 3]
                    row = ((group * 3 + tile) * 9 + c) * 8
                    cross[row : row + 8, 0:F] = one + two
                    cross[row : row + 8, F : 2 * F] = three - one + two
        both = cross[...]
        upper = both.astype(jnp.bfloat16)
        lower = (both - upper.astype(jnp.float32)).astype(jnp.bfloat16)
        high = high_ref[...]
        product = jnp.dot(upper, low_ref[...], preferred_element_type=jnp.float32)
        product += jnp.dot(lower, high, preferred_element_type=jnp.float32)
        product += jnp.dot(upper, high, preferred_element_type=jnp.float32)
        lagged[...] = product
        for group in range(G):
            hits = (group_tile_ref[...] == group).astype(jnp.float32)
            scale = lax.rsqrt(jnp.sum(hits, keepdims=True))
            for q in range(4):
                to = owner_ref[4 * s + q]
                for c in range(9):
                    r = q * PB
                    while r < (q + 1) * PB:
                        tile, inside = divmod(r, 8)
                        count = min(8 - inside, (q + 1) * PB - r)
                        row = ((group * 3 + tile) * 9 + c) * 8 + inside
                        put = (group * 9 + c) * PB + r - q * PB
                        out_ref[to, put : put + count] = lagged[row : row + count] * scale
                        r += count
        return carry

    lax.fori_loop(0, S, one_source, 0)


def stack(day, group_of, owner, spectra, sources):
    high, low = lag_tables()
    vmem = pl.BlockSpec(memory_space=pltpu.VMEM)
    smem = pl.BlockSpec(memory_space=pltpu.SMEM)
    rec = pltpu.VMEM((SEG, 3, R, F), jnp.float32)
    src = pltpu.VMEM((SEG + 1, 6 * SB, F), jnp.float32)
    return pl.pallas_call(
        stack_kernel,
        out_shape=jax.ShapeDtypeStruct((N_DAY, ROWS, LAG), jnp.float32),
        in_specs=[smem, smem, smem, vmem, vmem, vmem, vmem, vmem],
        out_specs=vmem,
        scratch_shapes=[
            rec, rec, rec, src, src, src,
            pltpu.VMEM((G * 3 * 9 * 8, 2 * F), jnp.float32),
            pltpu.VMEM((G * 3 * 9 * 8, LAG), jnp.float32),
            pltpu.SMEM((G, SEG + UNROLL), jnp.int32),
        ],
        compiler_params=pltpu.CompilerParams(vmem_limit_bytes=VMEM_LIMIT),
        name="stack",
    )(
        day, group_of, owner, group_of.reshape(-1, 128), spectra, sources,
        jnp.asarray(high), jnp.asarray(low),
    )


def reduce_kernel(part_ref, out_ref, slots, y_mine, y_slots, z_send, z_recv, y_send, y_recv):
    day = lax.axis_index("day")
    z, y = day // N_Y, lax.rem(day, N_Y)

    def owner(dz, dy):
        return lax.rem(z + dz + N_Z, N_Z) * N_Y + lax.rem(y + dy, N_Y)

    barrier = pltpu.get_barrier_semaphore()
    partners = [owner(1, 0), owner(-1, 0)] + [owner(0, dy) for dy in range(1, N_Y)]
    for to in partners:
        pl.semaphore_signal(barrier, inc=1, device_id={"day": to}, device_id_type=MESH)
    pl.semaphore_wait(barrier, len(partners))

    half = N_Z // 2
    order = (2, 1, 3, 0)
    opening = ((2, 1), (3, 0))
    copies = {}

    def hop(way, step, dy, source):
        copy = pltpu.make_async_remote_copy(
            src_ref=source,
            dst_ref=slots.at[way, step, dy],
            send_sem=z_send.at[way, step, dy],
            recv_sem=z_recv.at[way, step, dy],
            device_id={"day": owner(1 - 2 * way, 0)},
            device_id_type=MESH,
        )
        copy.start()
        copies[way, step, dy] = copy

    for step in range(half):
        for dy in order:
            for way in range(2):
                dz = (half - step) * (1 - 2 * way)
                own = owner(dz, dy)
                if step == 0:
                    if dy in opening[way]:
                        hop(way, step, dy, part_ref.at[own])
                elif (way, step - 1, dy) in copies:
                    copies[way, step - 1, dy].wait_recv()
                    slots[way, step - 1, dy] += part_ref[own]
                    hop(way, step, dy, slots.at[way, step - 1, dy])
                else:
                    hop(way, step, dy, part_ref.at[own])
    y_copies = []
    for dy in order:
        for way in range(2):
            copies[way, half - 1, dy].wait_recv()
        total = part_ref[owner(0, dy)] + slots[0, half - 1, dy] + slots[1, half - 1, dy]
        y_mine[dy] = total
        if dy:
            copy = pltpu.make_async_remote_copy(
                src_ref=y_mine.at[dy],
                dst_ref=y_slots.at[dy - 1],
                send_sem=y_send.at[dy - 1],
                recv_sem=y_recv.at[dy - 1],
                device_id={"day": owner(0, dy)},
                device_id_type=MESH,
            )
            copy.start()
            y_copies.append(copy)
    for copy in y_copies:
        copy.wait_recv()
    total = y_mine[0] + y_slots[0] + y_slots[1] + y_slots[2]
    for group in range(G):
        for c in range(9):
            row = (group * 9 + c) * PB
            for r in range(PB):
                out_ref[r, c, group : group + 1, :] = total[row + r : row + r + 1]
    for copy in list(copies.values()) + y_copies:
        copy.wait_send()


def reduce(part):
    half = N_Z // 2
    chunk = (ROWS, LAG)
    return pl.pallas_call(
        reduce_kernel,
        out_shape=jax.ShapeDtypeStruct((PB, 9, G, LAG), jnp.float32),
        in_specs=[pl.BlockSpec(memory_space=pltpu.VMEM)],
        out_specs=pl.BlockSpec(memory_space=pltpu.VMEM),
        scratch_shapes=[
            pltpu.VMEM((2, half, N_Y) + chunk, jnp.float32),
            pltpu.VMEM((N_Y,) + chunk, jnp.float32),
            pltpu.VMEM((N_Y - 1,) + chunk, jnp.float32),
            pltpu.SemaphoreType.DMA((2, half, N_Y)),
            pltpu.SemaphoreType.DMA((2, half, N_Y)),
            pltpu.SemaphoreType.DMA((N_Y - 1,)),
            pltpu.SemaphoreType.DMA((N_Y - 1,)),
        ],
        compiler_params=pltpu.CompilerParams(
            collective_id=1, has_side_effects=True, vmem_limit_bytes=VMEM_LIMIT
        ),
        name="reduce",
    )(part)


def local(spectra, src_block, group_of, owner):
    sources = share(src_block, spectra)
    day = lax.axis_index("day").astype(jnp.int32).reshape(1)
    part = stack(day, group_of, owner, spectra, sources)
    return reduce(part).transpose(0, 2, 1, 3)[None]


def solution(mesh):
    return jax.shard_map(
        local,
        mesh=mesh,
        in_specs=(P("day", None, None, "sta", None), P(), P(), P()),
        out_specs=P("day", "sta", None, None, None),
        check_vma=False,
    )
```

```python
import jax
import jax.numpy as jnp
import numpy as np
from jax import lax
from jax.experimental import pallas as pl
from jax.experimental.pallas import tpu as pltpu
from jax.sharding import PartitionSpec as P

F = 128
LAG = 128
G = 2
SB = 4
S = 8
PB = 6
SEG = 64
R = 24
N_STA = 16
N_DAY = 32
N_Z = 8
N_Y = 4
HALF_Z = N_Z // 2
PIECE = SEG // N_STA
CHUNK = 4
N_CHUNK = SEG // CHUNK + 1
ROWS = 40
MESH = pl.DeviceIdType.MESH
VMEM_LIMIT = 56 * 1024 * 1024


def lag_tables():
    freq = np.arange(F)
    lag = np.arange(LAG) - LAG // 2
    angle = 2.0 * np.pi / (2 * F) * np.mod(freq[:, None] * lag[None, :], 2 * F)
    weight = np.where(freq == 0, 1.0, 2.0) / np.sqrt(F)
    table = np.concatenate(
        [weight[:, None] * np.cos(angle), -weight[:, None] * np.sin(angle)], axis=0
    )
    high = table.astype(jnp.bfloat16)
    low = (table - high.astype(np.float64)).astype(jnp.bfloat16)
    return np.concatenate([high, low], axis=1)


def plan_kernel(day_ref, group_ref, owner_ref, tile_ref, order_ref, block_ref, scale_ref):
    first = day_ref[0] * SEG

    def clear(i, carry):
        order_ref[i] = SEG
        return carry

    lax.fori_loop(0, N_CHUNK * CHUNK, clear, 0)
    ones = lax.fori_loop(0, SEG, lambda t, n: n + group_ref[first + t], jnp.int32(0))
    chunks = (SEG - ones + CHUNK - 1) // CHUNK
    order_ref[N_CHUNK * CHUNK] = chunks

    def place(t, carry):
        early, late = carry
        group = group_ref[first + t]
        order_ref[jnp.where(group == 0, early, late)] = t
        return early + 1 - group, late + group

    lax.fori_loop(0, SEG, place, (jnp.int32(0), chunks * CHUNK))

    def turn(k, carry):
        block_ref[owner_ref[k]] = k
        return carry

    lax.fori_loop(0, N_DAY, turn, 0)
    for group in range(G):
        hits = (tile_ref[...] == group).astype(jnp.float32)
        scale_ref[group] = jnp.broadcast_to(lax.rsqrt(jnp.sum(hits, keepdims=True)), (8, LAG))


def plan(day, group_of, owner):
    vmem = pl.BlockSpec(memory_space=pltpu.VMEM)
    smem = pl.BlockSpec(memory_space=pltpu.SMEM)
    return pl.pallas_call(
        plan_kernel,
        out_shape=(
            jax.ShapeDtypeStruct((N_CHUNK * CHUNK + 4,), jnp.int32),
            jax.ShapeDtypeStruct((N_DAY,), jnp.int32),
            jax.ShapeDtypeStruct((G, 8, LAG), jnp.float32),
        ),
        in_specs=[smem, smem, smem, vmem],
        out_specs=(smem, smem, vmem),
        name="plan",
    )(day, group_of, owner, group_of.reshape(-1, 128))


def main_kernel(
    root_ref, order_ref, block_ref, scale_ref, table_ref, spec_ref, out_ref,
    spec, mine, seen, picked, rec_re, rec_im, rec_sum, src_re, src_im, src_dif, hist, cross, part,
    opening, slots, y_mine, y_slots,
    in_sem, a_send, a_recv, b_send, b_recv, c_send, c_recv, z_send, z_recv, y_send, y_recv,
):
    me = lax.axis_index("sta")
    partner = me + 1 - 2 * lax.rem(me, 2)
    day = lax.axis_index("day")
    z, y = day // N_Y, lax.rem(day, N_Y)
    rec = (rec_re, rec_im, rec_sum)
    src = (src_re, src_im, src_dif)

    def member(dz, dy):
        return lax.rem(z + dz + N_Z, N_Z) * N_Y + lax.rem(y + dy, N_Y)

    def push(source, target, send, recv, device):
        return pltpu.make_async_remote_copy(
            src_ref=source, dst_ref=target, send_sem=send, recv_sem=recv,
            device_id=device, device_id_type=MESH,
        )

    started = []

    fetch = [
        pltpu.make_async_copy(
            spec_ref.at[:, :, :, :, pl.ds(at, n), :], spec.at[:, :, :, :, pl.ds(at, n), :], in_sem.at[i]
        )
        for i, (at, n) in enumerate(((0, 8), (8, R - 8)))
    ]
    for copy in fetch:
        copy.start()
    barrier = pltpu.get_barrier_semaphore()
    for step in range(1, N_STA):
        pl.semaphore_signal(
            barrier, inc=1, device_id={"sta": lax.rem(me + step, N_STA)}, device_id_type=MESH
        )
    near = [member(1, 0), member(-1, 0)] + [member(0, dy) for dy in range(1, N_Y)]
    for to in near:
        pl.semaphore_signal(barrier, inc=1, device_id={"day": to}, device_id_type=MESH)
    fetch[0].wait()
    for p in range(2):
        for comp in range(3):
            row = (p * 3 + comp) * SB
            mine[:, :, row : row + SB, :] = spec[:, :, p, comp, 0:SB, :]
    pl.semaphore_wait(barrier, N_STA - 1 + len(near))
    scatters = []
    for step in range(1, N_STA):
        to = lax.rem(me + step, N_STA)
        scatters.append(
            push(mine.at[to], seen.at[me], a_send.at[step - 1], a_recv.at[step - 1], {"sta": to})
        )
        scatters[-1].start()
    seen[me] = mine[me]
    fetch[1].wait()

    def widen_rec(j, carry):
        for i in range(PIECE):
            for comp in range(3):
                real = spec[j, i, 0, comp].astype(jnp.float32)
                imag = spec[j, i, 1, comp].astype(jnp.float32)
                rec_re[j * PIECE + i, comp] = real
                rec_im[j * PIECE + i, comp] = imag
                rec_sum[j * PIECE + i, comp] = real + imag
        return carry

    lax.fori_loop(0, N_STA, widen_rec, 0)
    for k in range(3):
        rec[k][SEG] = jnp.zeros((3, R, F), jnp.float32)
        src[k][SEG] = jnp.zeros((6 * SB, F), jnp.float32)
    hist[0] = jnp.zeros((3 * SB, 3, 8, F), jnp.float32)
    for copy in scatters:
        copy.wait_recv()
    for block in range(2):
        picked[me, block] = seen[root_ref[block]]
    half = N_STA // 2
    spreads, hands = [], []
    for step in range(1, half):
        to = lax.rem(me + 2 * step, N_STA)
        spreads.append(
            push(picked.at[me], picked.at[me], b_send.at[step - 1], b_recv.at[step - 1], {"sta": to})
        )
        spreads[-1].start()
    for step in range(half):
        if step:
            spreads[step - 1].wait_recv()
        piece = picked.at[lax.rem(me + N_STA - 2 * step, N_STA)]
        hands.append(push(piece, piece, c_send.at[step], c_recv.at[step], {"sta": partner}))
        hands[-1].start()
    for copy in hands:
        copy.wait_recv()
    started += scatters + spreads + hands

    def widen_src(j, carry):
        for i in range(PIECE):
            for block in range(2):
                rows = picked[j, block, i].astype(jnp.float32)
                real, imag = rows[: 3 * SB], rows[3 * SB :]
                at = pl.ds(block * 3 * SB, 3 * SB)
                src_re[j * PIECE + i, at] = real
                src_im[j * PIECE + i, at] = imag
                src_dif[j * PIECE + i, at] = real - imag
        return carry

    lax.fori_loop(0, N_STA, widen_src, 0)

    def unit(a, block, tile):
        place = pl.ds(tile * 8, 8)
        sums = [jnp.zeros((3, 8, F), jnp.float32)] * (3 * SB)
        for chunk in range(N_CHUNK):
            for turn in range(CHUNK):
                t = order_ref[chunk * CHUNK + turn]
                held = [rec[k][t, :, place] for k in range(3)]
                for s in range(SB):
                    row = pl.ds((block * 3 + a) * SB + s, 8, stride=0)
                    for k in range(3):
                        sums[s * 3 + k] = sums[s * 3 + k] + src[k][t, row][None] * held[k]
            for i in range(3 * SB):
                hist[chunk + 1, i] = sums[i]
        cut = order_ref[N_CHUNK * CHUNK]
        for s in range(SB):
            early = [hist[cut, 3 * s + k] for k in range(3)]
            late = [sums[3 * s + k] - early[k] for k in range(3)]
            for group, (one, two, three) in enumerate((early, late)):
                cross[group, s, :, :, 0:F] = one + two
                cross[group, s, :, :, F : 2 * F] = three - one + two
        both = cross[...].reshape(G * SB * 3 * 8, 2 * F)
        upper = both.astype(jnp.bfloat16)
        lower = (both - upper.astype(jnp.float32)).astype(jnp.bfloat16)
        wide = jnp.dot(upper, table_ref[...], preferred_element_type=jnp.float32)
        narrow = jnp.dot(lower, table_ref[:, 0:LAG], preferred_element_type=jnp.float32)
        lagged = (wide[:, :LAG] + wide[:, LAG:] + narrow).reshape(G, SB, 3, 8, LAG)
        for group in range(G):
            for s in range(SB):
                for b in range(3):
                    rows = lagged[group, s, b] * scale_ref[group]
                    r = tile * 8
                    while r < tile * 8 + 8:
                        q, inside = divmod(r, PB)
                        count = min(PB - inside, tile * 8 + 8 - r)
                        put = (group * 3 + b) * PB + inside
                        at = r - tile * 8
                        part[a, (block * SB + s) * 4 + q, put : put + count] = rows[at : at + count]
                        r += count

    def own(a, dz, dy):
        return part[a, block_ref[member(dz, dy)]]

    chains = {}

    def hop(a, step):
        for way in range(2):
            dz = (HALF_Z - step) * (1 - 2 * way)
            to = {"day": member(1 - 2 * way, 0)}
            sems = (z_send.at[a, way, step], z_recv.at[a, way, step])
            if step == 0:
                for i in range(2):
                    opening[a, way, i] = own(a, dz, 2 * way + i)
                copy = push(
                    opening.at[a, way], slots.at[a, way, 0, pl.ds(2 * way, 2)], *sems, to
                )
            else:
                chains[a, way, step - 1].wait_recv()
                for dy in range(N_Y):
                    if step == 1 and dy // 2 != way:
                        slots[a, way, 0, dy] = own(a, dz, dy)
                    else:
                        slots[a, way, step - 1, dy] += own(a, dz, dy)
                copy = push(slots.at[a, way, step - 1], slots.at[a, way, step], *sems, to)
            copy.start()
            chains[a, way, step] = copy
            started.append(copy)

    crossings = {}

    def across(a):
        for way in range(2):
            chains[a, way, HALF_Z - 1].wait_recv()
        for dy in (2, 1, 3, 0):
            y_mine[a, dy] = own(a, 0, dy) + slots[a, 0, HALF_Z - 1, dy] + slots[a, 1, HALF_Z - 1, dy]
            if dy:
                copy = push(
                    y_mine.at[a, dy], y_slots.at[a, dy - 1],
                    y_send.at[a, dy - 1], y_recv.at[a, dy - 1], {"day": member(0, dy)},
                )
                copy.start()
                crossings[a, dy] = copy
                started.append(copy)

    def finish(a):
        for dy in range(1, N_Y):
            crossings[a, dy].wait_recv()
        total = y_mine[a, 0] + y_slots[a, 0] + y_slots[a, 1] + y_slots[a, 2]
        for group in range(G):
            for b in range(3):
                row = (group * 3 + b) * PB
                for r in range(PB):
                    out_ref[r, 3 * a + b, group : group + 1, :] = total[row + r : row + r + 1]

    def twice(a, tile):
        def body(block, carry):
            unit(a, block, tile)
            return carry

        lax.fori_loop(0, 2, body, 0)

    for tile in range(3):
        twice(0, tile)
    hop(0, 0)
    twice(1, 0)
    hop(0, 1)
    twice(1, 1)
    hop(0, 2)
    twice(1, 2)
    hop(0, 3)
    hop(1, 0)
    twice(2, 0)
    hop(1, 1)
    across(0)
    twice(2, 1)
    hop(1, 2)
    finish(0)
    twice(2, 2)
    hop(2, 0)
    hop(1, 3)
    hop(2, 1)
    across(1)
    hop(2, 2)
    finish(1)
    hop(2, 3)
    across(2)
    finish(2)
    for copy in started:
        copy.wait_send()


def main(src_block, order, block_at, scale, spectra):
    pieces = spectra.reshape(N_STA, PIECE, 2, 3, R, F)
    half = N_STA // 2
    vmem = pl.BlockSpec(memory_space=pltpu.VMEM)
    smem = pl.BlockSpec(memory_space=pltpu.SMEM)
    dma = pltpu.SemaphoreType.DMA
    rec = pltpu.VMEM((SEG + 1, 3, R, F), jnp.float32)
    src = pltpu.VMEM((SEG + 1, 6 * SB, F), jnp.float32)
    rows = pltpu.VMEM((N_STA, PIECE, 6 * SB, F), jnp.bfloat16)
    chunk = (ROWS, LAG)
    return pl.pallas_call(
        main_kernel,
        out_shape=jax.ShapeDtypeStruct((PB, 9, G, LAG), jnp.float32),
        in_specs=[smem, smem, smem, vmem, vmem, pl.BlockSpec(memory_space=pl.ANY)],
        out_specs=vmem,
        scratch_shapes=[
            pltpu.VMEM(pieces.shape, jnp.bfloat16),
            rows, rows,
            pltpu.VMEM((N_STA, 2, PIECE, 6 * SB, F), jnp.bfloat16),
            rec, rec, rec, src, src, src,
            pltpu.VMEM((N_CHUNK + 1, 3 * SB, 3, 8, F), jnp.float32),
            pltpu.VMEM((G, SB, 3, 8, 2 * F), jnp.float32),
            pltpu.VMEM((3, N_DAY) + chunk, jnp.float32),
            pltpu.VMEM((3, 2, 2) + chunk, jnp.float32),
            pltpu.VMEM((3, 2, HALF_Z, N_Y) + chunk, jnp.float32),
            pltpu.VMEM((3, N_Y) + chunk, jnp.float32),
            pltpu.VMEM((3, N_Y - 1) + chunk, jnp.float32),
            dma((2,)),
            dma((N_STA - 1,)), dma((N_STA - 1,)),
            dma((half - 1,)), dma((half - 1,)),
            dma((half,)), dma((half,)),
            dma((3, 2, HALF_Z)), dma((3, 2, HALF_Z)),
            dma((3, N_Y - 1)), dma((3, N_Y - 1)),
        ],
        compiler_params=pltpu.CompilerParams(
            collective_id=0, has_side_effects=True, vmem_limit_bytes=VMEM_LIMIT
        ),
        name="main",
    )(src_block, order, block_at, scale, jnp.asarray(lag_tables()), pieces)


def local(spectra, src_block, group_of, owner):
    day = lax.axis_index("day").astype(jnp.int32).reshape(1)
    order, block_at, scale = plan(day, group_of, owner)
    return main(src_block, order, block_at, scale, spectra).transpose(0, 2, 1, 3)[None]


def solution(mesh):
    return jax.shard_map(
        local,
        mesh=mesh,
        in_specs=(P("day", None, None, "sta", None), P(), P(), P()),
        out_specs=P("day", "sta", None, None, None),
        check_vma=False,
    )
```

```python
import jax
import jax.numpy as jnp
import numpy as np
from jax import lax
from jax.experimental import pallas as pl
from jax.experimental.pallas import tpu as pltpu
from jax.sharding import PartitionSpec as P

F = 128
LAG = 128
G = 2
SB = 4
S = 8
PB = 6
SEG = 64
R = 24
N_STA = 16
N_DAY = 32
PIECE = SEG // N_STA
CHUNK = 4
N_CHUNK = SEG // CHUNK + 1
ROWS = 40
CODED = 36
STEPS = 256.0
PEAK = 32767.0
BATCH = 8
MESH = pl.DeviceIdType.MESH
VMEM_LIMIT = 56 * 1024 * 1024


def lag_tables():
    freq = np.arange(F)
    lag = np.arange(LAG) - LAG // 2
    angle = 2.0 * np.pi / (2 * F) * np.mod(freq[:, None] * lag[None, :], 2 * F)
    weight = np.where(freq == 0, 1.0, 2.0) / np.sqrt(F)
    table = np.concatenate(
        [weight[:, None] * np.cos(angle), -weight[:, None] * np.sin(angle)], axis=0
    )
    high = table.astype(jnp.bfloat16)
    low = (table - high.astype(np.float64)).astype(jnp.bfloat16)
    return np.concatenate([high, low], axis=1)


def plan_kernel(day_ref, group_ref, owner_ref, tile_ref, order_ref, block_ref, scale_ref):
    first = day_ref[0] * SEG

    def clear(i, carry):
        order_ref[i] = SEG
        return carry

    lax.fori_loop(0, N_CHUNK * CHUNK, clear, 0, unroll=True)
    ones = lax.fori_loop(0, SEG, lambda t, n: n + group_ref[first + t], jnp.int32(0), unroll=True)
    chunks = (SEG - ones + CHUNK - 1) // CHUNK
    order_ref[N_CHUNK * CHUNK] = chunks

    def place(t, carry):
        early, late = carry
        group = group_ref[first + t]
        order_ref[jnp.where(group == 0, early, late)] = t
        return early + 1 - group, late + group

    lax.fori_loop(0, SEG, place, (jnp.int32(0), chunks * CHUNK), unroll=True)

    def turn(k, carry):
        block_ref[owner_ref[k]] = k
        return carry

    lax.fori_loop(0, N_DAY, turn, 0, unroll=True)
    for group in range(G):
        hits = (tile_ref[...] == group).astype(jnp.float32)
        scale_ref[group] = jnp.broadcast_to(lax.rsqrt(jnp.sum(hits, keepdims=True)), (8, LAG))


def plan(day, group_of, owner):
    vmem = pl.BlockSpec(memory_space=pltpu.VMEM)
    smem = pl.BlockSpec(memory_space=pltpu.SMEM)
    return pl.pallas_call(
        plan_kernel,
        out_shape=(
            jax.ShapeDtypeStruct((N_CHUNK * CHUNK + 4,), jnp.int32),
            jax.ShapeDtypeStruct((N_DAY,), jnp.int32),
            jax.ShapeDtypeStruct((G, 8, LAG), jnp.float32),
        ),
        in_specs=[smem, smem, smem, vmem],
        out_specs=(smem, smem, vmem),
        name="plan",
    )(day, group_of, owner, group_of.reshape(-1, 128))


def main_kernel(
    root_ref, order_ref, block_ref, scale_ref, table_ref, spec_ref, out_ref,
    spec, mine, seen, picked, rec_re, rec_im, rec_sum, src_re, src_im, src_dif, hist, cross, part,
    coded, slots, in_sem, a_send, a_recv, b_send, b_recv, c_send, c_recv, d_send, d_recv,
):
    me = lax.axis_index("sta")
    partner = me + 1 - 2 * lax.rem(me, 2)
    day = lax.axis_index("day")
    rec = (rec_re, rec_im, rec_sum)
    src = (src_re, src_im, src_dif)

    def push(source, target, send, recv, device):
        return pltpu.make_async_remote_copy(
            src_ref=source, dst_ref=target, send_sem=send, recv_sem=recv,
            device_id=device, device_id_type=MESH,
        )

    started = []

    fetch = [
        pltpu.make_async_copy(
            spec_ref.at[:, :, :, :, pl.ds(at, n), :], spec.at[:, :, :, :, pl.ds(at, n), :], in_sem.at[i]
        )
        for i, (at, n) in enumerate(((0, 8), (8, R - 8)))
    ]
    for copy in fetch:
        copy.start()
    barrier = pltpu.get_barrier_semaphore()
    for step in range(1, N_STA):
        pl.semaphore_signal(
            barrier, inc=1, device_id={"sta": lax.rem(me + step, N_STA)}, device_id_type=MESH
        )
    for step in range(1, N_DAY):
        pl.semaphore_signal(
            barrier, inc=1, device_id={"day": lax.rem(day + step, N_DAY)}, device_id_type=MESH
        )
    fetch[0].wait()
    for p in range(2):
        for comp in range(3):
            row = (p * 3 + comp) * SB
            mine[:, :, row : row + SB, :] = spec[:, :, p, comp, 0:SB, :]
    pl.semaphore_wait(barrier, N_STA + N_DAY - 2)
    scatters = []
    for step in range(1, N_STA):
        to = lax.rem(me + step, N_STA)
        scatters.append(
            push(mine.at[to], seen.at[me], a_send.at[step - 1], a_recv.at[step - 1], {"sta": to})
        )
        scatters[-1].start()
    seen[me] = mine[me]
    fetch[1].wait()

    def widen_rec(j, carry):
        for i in range(PIECE):
            for comp in range(3):
                real = spec[j, i, 0, comp].astype(jnp.float32)
                imag = spec[j, i, 1, comp].astype(jnp.float32)
                rec_re[j * PIECE + i, comp] = real
                rec_im[j * PIECE + i, comp] = imag
                rec_sum[j * PIECE + i, comp] = real + imag
        return carry

    lax.fori_loop(0, N_STA, widen_rec, 0)
    for k in range(3):
        rec[k][SEG] = jnp.zeros((3, R, F), jnp.float32)
        src[k][SEG] = jnp.zeros((6 * SB, F), jnp.float32)
    hist[0] = jnp.zeros((3 * SB, 3, 8, F), jnp.float32)
    for copy in scatters:
        copy.wait_recv()
    for block in range(2):
        picked[me, block] = seen[root_ref[block]]
    half = N_STA // 2
    spreads, hands = [], []
    for step in range(1, half):
        to = lax.rem(me + 2 * step, N_STA)
        spreads.append(
            push(picked.at[me], picked.at[me], b_send.at[step - 1], b_recv.at[step - 1], {"sta": to})
        )
        spreads[-1].start()
    for step in range(half):
        if step:
            spreads[step - 1].wait_recv()
        piece = picked.at[lax.rem(me + N_STA - 2 * step, N_STA)]
        hands.append(push(piece, piece, c_send.at[step], c_recv.at[step], {"sta": partner}))
        hands[-1].start()
    for copy in hands:
        copy.wait_recv()
    started += scatters + spreads + hands

    def widen_src(j, carry):
        for i in range(PIECE):
            for block in range(2):
                rows = picked[j, block, i].astype(jnp.float32)
                real, imag = rows[: 3 * SB], rows[3 * SB :]
                at = pl.ds(block * 3 * SB, 3 * SB)
                src_re[j * PIECE + i, at] = real
                src_im[j * PIECE + i, at] = imag
                src_dif[j * PIECE + i, at] = real - imag
        return carry

    lax.fori_loop(0, N_STA, widen_src, 0)

    def unit(a, block, tile):
        place = pl.ds(tile * 8, 8)
        sums = [jnp.zeros((3, 8, F), jnp.float32)] * (3 * SB)
        for chunk in range(N_CHUNK):
            for turn in range(CHUNK):
                t = order_ref[chunk * CHUNK + turn]
                held = [rec[k][t, :, place] for k in range(3)]
                for s in range(SB):
                    row = pl.ds((block * 3 + a) * SB + s, 8, stride=0)
                    for k in range(3):
                        sums[s * 3 + k] = sums[s * 3 + k] + src[k][t, row][None] * held[k]
            for i in range(3 * SB):
                hist[chunk + 1, i] = sums[i]
        cut = order_ref[N_CHUNK * CHUNK]
        for s in range(SB):
            early = [hist[cut, 3 * s + k] for k in range(3)]
            late = [sums[3 * s + k] - early[k] for k in range(3)]
            for group, (one, two, three) in enumerate((early, late)):
                cross[group, s, :, :, 0:F] = one + two
                cross[group, s, :, :, F : 2 * F] = three - one + two
        both = cross[...].reshape(G * SB * 3 * 8, 2 * F)
        upper = both.astype(jnp.bfloat16)
        lower = (both - upper.astype(jnp.float32)).astype(jnp.bfloat16)
        wide = jnp.dot(upper, table_ref[...], preferred_element_type=jnp.float32)
        narrow = jnp.dot(lower, table_ref[:, 0:LAG], preferred_element_type=jnp.float32)
        lagged = (wide[:, :LAG] + wide[:, LAG:] + narrow).reshape(G, SB, 3, 8, LAG)
        for group in range(G):
            for s in range(SB):
                for b in range(3):
                    rows = lagged[group, s, b] * scale_ref[group]
                    r = tile * 8
                    while r < tile * 8 + 8:
                        q, inside = divmod(r, PB)
                        count = min(PB - inside, tile * 8 + 8 - r)
                        put = (group * 3 + b) * PB + inside
                        at = r - tile * 8
                        part[a, (block * SB + s) * 4 + q, put : put + count] = rows[at : at + count]
                        r += count

    lane = lax.broadcasted_iota(jnp.int32, (ROWS, LAG), 1)
    line = lax.broadcasted_iota(jnp.int32, (ROWS, LAG), 0)
    diagonal = lane == line

    def parcel(a, step):
        return push(
            coded.at[a, step - 1], slots.at[a, step - 1],
            d_send.at[a, step - 1], d_recv.at[a, step - 1],
            {"day": lax.rem(day + step, N_DAY)},
        )

    def post(a):
        for first in range(1, N_DAY, BATCH):
            steps = range(first, min(first + BATCH, N_DAY))
            for step in steps:
                rows = part[a, block_ref[lax.rem(day + step, N_DAY)]]
                largest = jnp.max(jnp.abs(rows), axis=1, keepdims=True)
                level = jnp.ceil(jnp.log2(jnp.maximum(largest, 1e-30)) * STEPS)
                values = rows * (jnp.exp2(level * (-1.0 / STEPS)) * PEAK)
                levels = jnp.sum(jnp.where(diagonal, level, 0.0), axis=0, keepdims=True)
                values = jnp.where(line == CODED, levels, values)
                coded[a, step - 1] = jnp.round(values).astype(jnp.int32).astype(jnp.int16)
            for step in steps:
                parcel(a, step).start()

    def finish(a):
        total = part[a, block_ref[day]]
        for first in range(1, N_DAY, BATCH):
            steps = range(first, min(first + BATCH, N_DAY))
            for step in steps:
                parcel(a, step).wait_recv()
            for step in steps:
                values = slots[a, step - 1].astype(jnp.int32).astype(jnp.float32)
                levels = jnp.where(diagonal, values[CODED : CODED + 1], 0.0)
                level = jnp.sum(levels, axis=1, keepdims=True)
                total = total + values * (jnp.exp2(level * (1.0 / STEPS)) * (1.0 / PEAK))
        for group in range(G):
            for b in range(3):
                row = (group * 3 + b) * PB
                for r in range(PB):
                    out_ref[r, 3 * a + b, group : group + 1, :] = total[row + r : row + r + 1]

    def twice(a, tile):
        def body(block, carry):
            unit(a, block, tile)
            return carry

        lax.fori_loop(0, 2, body, 0)

    for a in range(3):
        for tile in range(3):
            twice(a, tile)
        post(a)
    for a in range(3):
        finish(a)
    for copy in started:
        copy.wait_send()

    def settle(j, carry):
        for a in range(3):
            parcel(a, 1 + j).wait_send()
        return carry

    lax.fori_loop(0, N_DAY - 1, settle, 0)


def main(src_block, order, block_at, scale, spectra):
    pieces = spectra.reshape(N_STA, PIECE, 2, 3, R, F)
    half = N_STA // 2
    vmem = pl.BlockSpec(memory_space=pltpu.VMEM)
    smem = pl.BlockSpec(memory_space=pltpu.SMEM)
    dma = pltpu.SemaphoreType.DMA
    rec = pltpu.VMEM((SEG + 1, 3, R, F), jnp.float32)
    src = pltpu.VMEM((SEG + 1, 6 * SB, F), jnp.float32)
    rows = pltpu.VMEM((N_STA, PIECE, 6 * SB, F), jnp.bfloat16)
    chunk = (ROWS, LAG)
    return pl.pallas_call(
        main_kernel,
        out_shape=jax.ShapeDtypeStruct((PB, 9, G, LAG), jnp.float32),
        in_specs=[smem, smem, smem, vmem, vmem, pl.BlockSpec(memory_space=pl.ANY)],
        out_specs=vmem,
        scratch_shapes=[
            pltpu.VMEM(pieces.shape, jnp.bfloat16),
            rows, rows,
            pltpu.VMEM((N_STA, 2, PIECE, 6 * SB, F), jnp.bfloat16),
            rec, rec, rec, src, src, src,
            pltpu.VMEM((N_CHUNK + 1, 3 * SB, 3, 8, F), jnp.float32),
            pltpu.VMEM((G, SB, 3, 8, 2 * F), jnp.float32),
            pltpu.VMEM((3, N_DAY) + chunk, jnp.float32),
            pltpu.VMEM((3, N_DAY - 1) + chunk, jnp.int16),
            pltpu.VMEM((3, N_DAY - 1) + chunk, jnp.int16),
            dma((2,)),
            dma((N_STA - 1,)), dma((N_STA - 1,)),
            dma((half - 1,)), dma((half - 1,)),
            dma((half,)), dma((half,)),
            dma((3, N_DAY - 1)), dma((3, N_DAY - 1)),
        ],
        compiler_params=pltpu.CompilerParams(
            collective_id=0, has_side_effects=True, vmem_limit_bytes=VMEM_LIMIT
        ),
        name="main",
    )(src_block, order, block_at, scale, jnp.asarray(lag_tables()), pieces)


def local(spectra, src_block, group_of, owner):
    day = lax.axis_index("day").astype(jnp.int32).reshape(1)
    order, block_at, scale = plan(day, group_of, owner)
    return main(src_block, order, block_at, scale, spectra).transpose(0, 2, 1, 3)[None]


def solution(mesh):
    return jax.shard_map(
        local,
        mesh=mesh,
        in_specs=(P("day", None, None, "sta", None), P(), P(), P()),
        out_specs=P("day", "sta", None, None, None),
        check_vma=False,
    )
```

```python
import jax
import jax.numpy as jnp
import numpy as np
from jax import lax
from jax.experimental import pallas as pl
from jax.experimental.pallas import tpu as pltpu
from jax.sharding import PartitionSpec as P

F = 128
LAG = 128
G = 2
SB = 4
S = 8
PB = 6
SEG = 64
R = 24
N_STA = 16
N_DAY = 32
PIECE = SEG // N_STA
CHUNK = 4
N_CHUNK = SEG // CHUNK + 1
PAIR = G * PB
ROUNDS = ((0, 1), (2, 3), (4, 5), (6, 7), (8,))
ROWS = 2 * PAIR
LAST = 16
STEPS = 256.0
PEAK = 32767.0
BATCH = 8
MESH = pl.DeviceIdType.MESH
VMEM_LIMIT = 56 * 1024 * 1024


def lag_tables():
    freq = np.arange(F)
    lag = np.arange(LAG) - LAG // 2
    angle = 2.0 * np.pi / (2 * F) * np.mod(freq[:, None] * lag[None, :], 2 * F)
    weight = np.where(freq == 0, 1.0, 2.0) / np.sqrt(F)
    table = np.concatenate(
        [weight[:, None] * np.cos(angle), -weight[:, None] * np.sin(angle)], axis=0
    )
    high = table.astype(jnp.bfloat16)
    low = (table - high.astype(np.float64)).astype(jnp.bfloat16)
    return np.concatenate([high, low], axis=1)


def plan_kernel(day_ref, group_ref, owner_ref, tile_ref, order_ref, block_ref, scale_ref):
    first = day_ref[0] * SEG

    def clear(i, carry):
        order_ref[i] = SEG
        return carry

    lax.fori_loop(0, N_CHUNK * CHUNK, clear, 0, unroll=True)
    ones = lax.fori_loop(0, SEG, lambda t, n: n + group_ref[first + t], jnp.int32(0), unroll=True)
    chunks = (SEG - ones + CHUNK - 1) // CHUNK
    order_ref[N_CHUNK * CHUNK] = chunks

    def place(t, carry):
        early, late = carry
        group = group_ref[first + t]
        order_ref[jnp.where(group == 0, early, late)] = t
        return early + 1 - group, late + group

    lax.fori_loop(0, SEG, place, (jnp.int32(0), chunks * CHUNK), unroll=True)

    def turn(k, carry):
        block_ref[owner_ref[k]] = k
        return carry

    lax.fori_loop(0, N_DAY, turn, 0, unroll=True)
    for group in range(G):
        hits = (tile_ref[...] == group).astype(jnp.float32)
        scale_ref[group] = jnp.broadcast_to(lax.rsqrt(jnp.sum(hits, keepdims=True)), (8, LAG))


def plan(day, group_of, owner):
    vmem = pl.BlockSpec(memory_space=pltpu.VMEM)
    smem = pl.BlockSpec(memory_space=pltpu.SMEM)
    return pl.pallas_call(
        plan_kernel,
        out_shape=(
            jax.ShapeDtypeStruct((N_CHUNK * CHUNK + 4,), jnp.int32),
            jax.ShapeDtypeStruct((N_DAY,), jnp.int32),
            jax.ShapeDtypeStruct((G, 8, LAG), jnp.float32),
        ),
        in_specs=[smem, smem, smem, vmem],
        out_specs=(smem, smem, vmem),
        name="plan",
    )(day, group_of, owner, group_of.reshape(-1, 128))


def main_kernel(
    root_ref, order_ref, block_ref, scale_ref, table_ref, spec_ref, out_ref,
    spec, mine, seen, picked, rec_re, rec_im, rec_sum, src_re, src_im, src_dif, hist, cross, part,
    coded, slots, coded_last, slots_last, levels, in_sem, a_send, a_recv, b_send, b_recv, c_send, c_recv, d_send, d_recv,
):
    me = lax.axis_index("sta")
    partner = me + 1 - 2 * lax.rem(me, 2)
    day = lax.axis_index("day")
    rec = (rec_re, rec_im, rec_sum)
    src = (src_re, src_im, src_dif)

    def push(source, target, send, recv, device):
        return pltpu.make_async_remote_copy(
            src_ref=source, dst_ref=target, send_sem=send, recv_sem=recv,
            device_id=device, device_id_type=MESH,
        )

    started = []

    fetch = [
        pltpu.make_async_copy(
            spec_ref.at[:, :, :, :, pl.ds(at, n), :], spec.at[:, :, :, :, pl.ds(at, n), :], in_sem.at[i]
        )
        for i, (at, n) in enumerate(((0, 8), (8, R - 8)))
    ]
    for copy in fetch:
        copy.start()
    barrier = pltpu.get_barrier_semaphore()
    for step in range(1, N_STA):
        pl.semaphore_signal(
            barrier, inc=1, device_id={"sta": lax.rem(me + step, N_STA)}, device_id_type=MESH
        )
    for step in range(1, N_DAY):
        pl.semaphore_signal(
            barrier, inc=1, device_id={"day": lax.rem(day + step, N_DAY)}, device_id_type=MESH
        )
    fetch[0].wait()
    for p in range(2):
        for comp in range(3):
            row = (p * 3 + comp) * SB
            mine[:, :, row : row + SB, :] = spec[:, :, p, comp, 0:SB, :]
    pl.semaphore_wait(barrier, N_STA + N_DAY - 2)
    scatters = []
    for step in range(1, N_STA):
        to = lax.rem(me + step, N_STA)
        scatters.append(
            push(mine.at[to], seen.at[me], a_send.at[step - 1], a_recv.at[step - 1], {"sta": to})
        )
        scatters[-1].start()
    seen[me] = mine[me]
    fetch[1].wait()

    def widen_rec(j, carry):
        for i in range(PIECE):
            for comp in range(3):
                real = spec[j, i, 0, comp].astype(jnp.float32)
                imag = spec[j, i, 1, comp].astype(jnp.float32)
                rec_re[j * PIECE + i, comp] = real
                rec_im[j * PIECE + i, comp] = imag
                rec_sum[j * PIECE + i, comp] = real + imag
        return carry

    lax.fori_loop(0, N_STA, widen_rec, 0)
    for k in range(3):
        rec[k][SEG] = jnp.zeros((3, R, F), jnp.float32)
        src[k][SEG] = jnp.zeros((6 * SB, F), jnp.float32)
    hist[0] = jnp.zeros((3 * SB, R, F), jnp.float32)
    for copy in scatters:
        copy.wait_recv()
    for block in range(2):
        picked[me, block] = seen[root_ref[block]]
    half = N_STA // 2

    def spread(block, step):
        piece = picked.at[me, block]
        to = lax.rem(me + 2 * step, N_STA)
        return push(piece, piece, b_send.at[block, step - 1], b_recv.at[block, step - 1], {"sta": to})

    def hand(block, step):
        piece = picked.at[lax.rem(me + N_STA - 2 * step, N_STA), block]
        return push(piece, piece, c_send.at[block, step], c_recv.at[block, step], {"sta": partner})

    spreads = [[spread(block, step) for step in range(1, half)] for block in range(2)]
    hands = [[hand(block, step) for step in range(half)] for block in range(2)]
    for block in range(2):
        for copy in spreads[block]:
            copy.start()
    started += scatters + spreads[0] + spreads[1] + hands[0] + hands[1]

    def hand_over(block):
        hands[block][0].start()
        for step in range(1, half):
            spreads[block][step - 1].wait_recv()
            hands[block][step].start()

    def take(block):
        for copy in hands[block]:
            copy.wait_recv()

        def widen_src(j, carry):
            for i in range(PIECE):
                rows = picked[j, block, i].astype(jnp.float32)
                real, imag = rows[: 3 * SB], rows[3 * SB :]
                at = pl.ds(block * 3 * SB, 3 * SB)
                src_re[j * PIECE + i, at] = real
                src_im[j * PIECE + i, at] = imag
                src_dif[j * PIECE + i, at] = real - imag
            return carry

        lax.fori_loop(0, N_STA, widen_src, 0)

    def unit(pair, block):
        a, b = divmod(pair, 3)
        sums = [jnp.zeros((R, F), jnp.float32)] * (3 * SB)
        for chunk in range(N_CHUNK):
            for turn in range(CHUNK):
                t = order_ref[chunk * CHUNK + turn]
                held = [rec[k][t, b].reshape(3, 8, F) for k in range(3)]
                for s in range(SB):
                    row = pl.ds((block * 3 + a) * SB + s, 8, stride=0)
                    for k in range(3):
                        product = src[k][t, row][None] * held[k]
                        sums[s * 3 + k] = sums[s * 3 + k] + product.reshape(R, F)
            for i in range(3 * SB):
                hist[chunk + 1, i] = sums[i]
        cut = order_ref[N_CHUNK * CHUNK]
        for s in range(SB):
            early = [hist[cut, 3 * s + k] for k in range(3)]
            late = [sums[3 * s + k] - early[k] for k in range(3)]
            for group, (one, two, three) in enumerate((early, late)):
                cross[group, s, :, 0:F] = one + two
                cross[group, s, :, F : 2 * F] = three - one + two
        both = cross[...].reshape(G * SB * R, 2 * F)
        upper = both.astype(jnp.bfloat16)
        lower = (both - upper.astype(jnp.float32)).astype(jnp.bfloat16)
        wide = jnp.dot(upper, table_ref[...], preferred_element_type=jnp.float32)
        narrow = jnp.dot(lower, table_ref[:, 0:LAG], preferred_element_type=jnp.float32)
        lagged = (wide[:, :LAG] + wide[:, LAG:] + narrow).reshape(G, SB, R, LAG)
        for group in range(G):
            scale = scale_ref[group, 0:1]
            put = (pair % 2 * G + group) * PB
            for s in range(SB):
                rows = lagged[group, s] * scale
                for q in range(R // PB):
                    part[pair // 2, (block * SB + s) * 4 + q, put : put + PB] = rows[q * PB : (q + 1) * PB]

    lane = lax.broadcasted_iota(jnp.int32, (ROWS, LAG), 1)
    line = lax.broadcasted_iota(jnp.int32, (ROWS, LAG), 0)
    end = len(ROUNDS) - 1
    height = [ROWS] * end + [LAST]
    diagonal = [(lane == line + n * ROWS)[: height[n]] for n in range(end + 1)]

    def parcel(n, step):
        source, target = (coded_last, slots_last) if n == end else (coded.at[n], slots.at[n])
        return push(
            source.at[step - 1], target.at[step - 1], d_send.at[n, step - 1], d_recv.at[n, step - 1],
            {"day": lax.rem(day + step, N_DAY)},
        )

    def post(n):
        for first in range(1, N_DAY, BATCH):
            steps = range(first, min(first + BATCH, N_DAY))
            for step in steps:
                rows = part[n, block_ref[lax.rem(day + step, N_DAY)], 0 : height[n]]
                largest = jnp.max(jnp.abs(rows), axis=1, keepdims=True)
                level = jnp.ceil(jnp.log2(jnp.maximum(largest, 1e-30)) * STEPS)
                values = rows * (jnp.exp2(level * (-1.0 / STEPS)) * PEAK)
                if n == end:
                    level, at = level[:PAIR], diagonal[n][:PAIR]
                else:
                    at = diagonal[n]
                mine_levels = jnp.sum(jnp.where(at, level, 0.0), axis=0, keepdims=True)
                if n:
                    mine_levels += levels[step - 1]
                if n < end:
                    levels[step - 1] = mine_levels
                    coded[n, step - 1] = jnp.round(values).astype(jnp.int32).astype(jnp.int16)
                else:
                    values = jnp.where(line[:LAST] == PAIR, mine_levels, values)
                    coded_last[step - 1] = jnp.round(values).astype(jnp.int32).astype(jnp.int16)
            for step in steps:
                parcel(n, step).start()

    def finish():
        totals = [part[n, block_ref[day], 0 : height[n]] for n in range(end + 1)]
        for first in range(1, N_DAY, BATCH):
            steps = range(first, min(first + BATCH, N_DAY))
            for step in steps:
                for n in range(end + 1):
                    parcel(n, step).wait_recv()
            for step in steps:
                values = [slots[n, step - 1] for n in range(end)] + [slots_last[step - 1]]
                values = [v.astype(jnp.int32).astype(jnp.float32) for v in values]
                coding = values[end][PAIR : PAIR + 1]
                for n in range(end + 1):
                    level = jnp.sum(jnp.where(diagonal[n], coding, 0.0), axis=1, keepdims=True)
                    totals[n] += values[n] * (jnp.exp2(level * (1.0 / STEPS)) * (1.0 / PEAK))
        for pair in range(9):
            for group in range(G):
                row = (pair % 2 * G + group) * PB
                for r in range(PB):
                    out_ref[r, pair, group : group + 1, :] = totals[pair // 2][row + r : row + r + 1]

    def twice(pair):
        def body(block, carry):
            unit(pair, block)
            return carry

        lax.fori_loop(0, 2, body, 0)

    hand_over(0)
    take(0)
    hand_over(1)
    for pair in ROUNDS[0]:
        unit(pair, 0)
    take(1)
    for pair in ROUNDS[0]:
        unit(pair, 1)
    post(0)
    for n in range(1, end + 1):
        for pair in ROUNDS[n]:
            twice(pair)
        post(n)
    finish()
    for copy in started:
        copy.wait_send()

    def settle(j, carry):
        for n in range(end + 1):
            parcel(n, 1 + j).wait_send()
        return carry

    lax.fori_loop(0, N_DAY - 1, settle, 0)


def main(src_block, order, block_at, scale, spectra):
    pieces = spectra.reshape(N_STA, PIECE, 2, 3, R, F)
    half = N_STA // 2
    vmem = pl.BlockSpec(memory_space=pltpu.VMEM)
    smem = pl.BlockSpec(memory_space=pltpu.SMEM)
    dma = pltpu.SemaphoreType.DMA
    rec = pltpu.VMEM((SEG + 1, 3, R, F), jnp.float32)
    src = pltpu.VMEM((SEG + 1, 6 * SB, F), jnp.float32)
    rows = pltpu.VMEM((N_STA, PIECE, 6 * SB, F), jnp.bfloat16)
    coded = pltpu.VMEM((len(ROUNDS) - 1, N_DAY - 1, ROWS, LAG), jnp.int16)
    last = pltpu.VMEM((N_DAY - 1, LAST, LAG), jnp.int16)
    return pl.pallas_call(
        main_kernel,
        out_shape=jax.ShapeDtypeStruct((PB, 9, G, LAG), jnp.float32),
        in_specs=[smem, smem, smem, vmem, vmem, pl.BlockSpec(memory_space=pl.ANY)],
        out_specs=vmem,
        scratch_shapes=[
            pltpu.VMEM(pieces.shape, jnp.bfloat16),
            rows, rows,
            pltpu.VMEM((N_STA, 2, PIECE, 6 * SB, F), jnp.bfloat16),
            rec, rec, rec, src, src, src,
            pltpu.VMEM((N_CHUNK + 1, 3 * SB, R, F), jnp.float32),
            pltpu.VMEM((G, SB, R, 2 * F), jnp.float32),
            pltpu.VMEM((len(ROUNDS), N_DAY, ROWS, LAG), jnp.float32),
            coded, coded, last, last,
            pltpu.VMEM((N_DAY - 1, 1, LAG), jnp.float32),
            dma((2,)),
            dma((N_STA - 1,)), dma((N_STA - 1,)),
            dma((2, half - 1)), dma((2, half - 1)),
            dma((2, half)), dma((2, half)),
            dma((len(ROUNDS), N_DAY - 1)), dma((len(ROUNDS), N_DAY - 1)),
        ],
        compiler_params=pltpu.CompilerParams(
            collective_id=0, has_side_effects=True, vmem_limit_bytes=VMEM_LIMIT
        ),
        name="main",
    )(src_block, order, block_at, scale, jnp.asarray(lag_tables()), pieces)


def local(spectra, src_block, group_of, owner):
    day = lax.axis_index("day").astype(jnp.int32).reshape(1)
    order, block_at, scale = plan(day, group_of, owner)
    return main(src_block, order, block_at, scale, spectra).transpose(0, 2, 1, 3)[None]


def solution(mesh):
    return jax.shard_map(
        local,
        mesh=mesh,
        in_specs=(P("day", None, None, "sta", None), P(), P(), P()),
        out_specs=P("day", "sta", None, None, None),
        check_vma=False,
    )
```

```python
import jax
import jax.numpy as jnp
import numpy as np
from jax import lax
from jax.experimental import pallas as pl
from jax.experimental.pallas import tpu as pltpu
from jax.sharding import PartitionSpec as P

F = 128
LAG = 128
G = 2
SB = 4
S = 8
PB = 6
SEG = 64
R = 24
N_STA = 16
N_DAY = 32
PIECE = SEG // N_STA
CHUNK = 4
N_CHUNK = SEG // CHUNK + 1
PAIR = G * PB
ROUNDS = ((0, 1), (2, 3), (4, 5), (6, 7), (8,))
ROWS = 2 * PAIR
LAST = 16
STEPS = 256.0
PEAK = 32767.0
BATCH = 8


def both_ways(count):
    ups = range(count // 2, 0, -1)
    return [step for up in ups for step in ((up, count - up) if 2 * up < count else (up,))]


MESH = pl.DeviceIdType.MESH
VMEM_LIMIT = 56 * 1024 * 1024


def lag_tables():
    freq = np.arange(F)
    lag = np.arange(LAG) - LAG // 2
    angle = 2.0 * np.pi / (2 * F) * np.mod(freq[:, None] * lag[None, :], 2 * F)
    weight = np.where(freq == 0, 1.0, 2.0) / np.sqrt(F)
    table = np.concatenate(
        [weight[:, None] * np.cos(angle), -weight[:, None] * np.sin(angle)], axis=0
    )
    high = table.astype(jnp.bfloat16)
    low = (table - high.astype(np.float64)).astype(jnp.bfloat16)
    return np.concatenate([high, low], axis=1)


def plan_kernel(day_ref, group_ref, owner_ref, tile_ref, order_ref, block_ref, scale_ref):
    first = day_ref[0] * SEG

    def clear(i, carry):
        order_ref[i] = SEG
        return carry

    lax.fori_loop(0, N_CHUNK * CHUNK, clear, 0, unroll=True)
    ones = lax.fori_loop(0, SEG, lambda t, n: n + group_ref[first + t], jnp.int32(0), unroll=True)
    chunks = (SEG - ones + CHUNK - 1) // CHUNK
    order_ref[N_CHUNK * CHUNK] = chunks

    def place(t, carry):
        early, late = carry
        group = group_ref[first + t]
        order_ref[jnp.where(group == 0, early, late)] = t
        return early + 1 - group, late + group

    lax.fori_loop(0, SEG, place, (jnp.int32(0), chunks * CHUNK), unroll=True)

    def turn(k, carry):
        block_ref[owner_ref[k]] = k
        return carry

    lax.fori_loop(0, N_DAY, turn, 0, unroll=True)
    for group in range(G):
        hits = (tile_ref[...] == group).astype(jnp.float32)
        scale_ref[group] = jnp.broadcast_to(lax.rsqrt(jnp.sum(hits, keepdims=True)), (8, LAG))


def plan(day, group_of, owner):
    vmem = pl.BlockSpec(memory_space=pltpu.VMEM)
    smem = pl.BlockSpec(memory_space=pltpu.SMEM)
    return pl.pallas_call(
        plan_kernel,
        out_shape=(
            jax.ShapeDtypeStruct((N_CHUNK * CHUNK + 4,), jnp.int32),
            jax.ShapeDtypeStruct((N_DAY,), jnp.int32),
            jax.ShapeDtypeStruct((G, 8, LAG), jnp.float32),
        ),
        in_specs=[smem, smem, smem, vmem],
        out_specs=(smem, smem, vmem),
        name="plan",
    )(day, group_of, owner, group_of.reshape(-1, 128))


def main_kernel(
    root_ref, order_ref, block_ref, scale_ref, table_ref, spec_ref, out_ref,
    spec, mine, seen, picked, rec_re, rec_im, rec_sum, src_re, src_im, src_dif, hist, cross, part,
    coded, slots, coded_last, slots_last, levels, in_sem, a_send, a_recv, b_send, b_recv, c_send, c_recv, d_send, d_recv,
):
    me = lax.axis_index("sta")
    partner = me + 1 - 2 * lax.rem(me, 2)
    day = lax.axis_index("day")
    rec = (rec_re, rec_im, rec_sum)
    src = (src_re, src_im, src_dif)

    def push(source, target, send, recv, device):
        return pltpu.make_async_remote_copy(
            src_ref=source, dst_ref=target, send_sem=send, recv_sem=recv,
            device_id=device, device_id_type=MESH,
        )

    started = []

    fetch = [
        pltpu.make_async_copy(
            spec_ref.at[:, :, :, :, pl.ds(at, n), :], spec.at[:, :, :, :, pl.ds(at, n), :], in_sem.at[i]
        )
        for i, (at, n) in enumerate(((0, 8), (8, R - 8)))
    ]
    for copy in fetch:
        copy.start()
    barrier = pltpu.get_barrier_semaphore()
    for step in range(1, N_STA):
        pl.semaphore_signal(
            barrier, inc=1, device_id={"sta": lax.rem(me + step, N_STA)}, device_id_type=MESH
        )
    for step in range(1, N_DAY):
        pl.semaphore_signal(
            barrier, inc=1, device_id={"day": lax.rem(day + step, N_DAY)}, device_id_type=MESH
        )
    fetch[0].wait()
    for p in range(2):
        for comp in range(3):
            row = (p * 3 + comp) * SB
            mine[:, :, row : row + SB, :] = spec[:, :, p, comp, 0:SB, :]
    pl.semaphore_wait(barrier, N_STA + N_DAY - 2)
    scatters = []
    for step in both_ways(N_STA):
        to = lax.rem(me + step, N_STA)
        scatters.append(
            push(mine.at[to], seen.at[me], a_send.at[step - 1], a_recv.at[step - 1], {"sta": to})
        )
        scatters[-1].start()
    seen[me] = mine[me]
    fetch[1].wait()

    def widen_rec(j, carry):
        for i in range(PIECE):
            for comp in range(3):
                real = spec[j, i, 0, comp].astype(jnp.float32)
                imag = spec[j, i, 1, comp].astype(jnp.float32)
                rec_re[j * PIECE + i, comp] = real
                rec_im[j * PIECE + i, comp] = imag
                rec_sum[j * PIECE + i, comp] = real + imag
        return carry

    lax.fori_loop(0, N_STA, widen_rec, 0)
    for k in range(3):
        rec[k][SEG] = jnp.zeros((3, R, F), jnp.float32)
        src[k][SEG] = jnp.zeros((2, 3 * SB, F), jnp.float32)
    hist[0] = jnp.zeros((3 * SB, R, F), jnp.float32)
    for copy in scatters:
        copy.wait_recv()
    for block in range(2):
        picked[me, block] = seen[root_ref[block]]
    half = N_STA // 2

    def spread(block, step):
        piece = picked.at[me, block]
        to = lax.rem(me + 2 * step, N_STA)
        return push(piece, piece, b_send.at[block, step - 1], b_recv.at[block, step - 1], {"sta": to})

    def hand(block, step):
        piece = picked.at[lax.rem(me + N_STA - 2 * step, N_STA), block]
        return push(piece, piece, c_send.at[block, step], c_recv.at[block, step], {"sta": partner})

    turns = both_ways(half)
    spreads = [[spread(block, step) for step in turns] for block in range(2)]
    hands = [[hand(block, step) for step in range(half)] for block in range(2)]
    for block in range(2):
        for copy in spreads[block]:
            copy.start()
    started += scatters + spreads[0] + spreads[1] + hands[0] + hands[1]

    def hand_over(block):
        hands[block][0].start()
        for i, step in enumerate(turns):
            spreads[block][i].wait_recv()
            hands[block][step].start()

    def take(block):
        for copy in hands[block]:
            copy.wait_recv()

        def widen_src(j, carry):
            for i in range(PIECE):
                rows = picked[j, block, i].astype(jnp.float32)
                real, imag = rows[: 3 * SB], rows[3 * SB :]
                src_re[j * PIECE + i, block] = real
                src_im[j * PIECE + i, block] = imag
                src_dif[j * PIECE + i, block] = real - imag
            return carry

        lax.fori_loop(0, N_STA, widen_src, 0)

    def unit(pair, block):
        a, b = divmod(pair, 3)
        sums = [jnp.zeros((R, F), jnp.float32)] * (3 * SB)
        for chunk in range(N_CHUNK):
            for turn in range(CHUNK):
                t = order_ref[chunk * CHUNK + turn]
                held = [rec[k][t, b].reshape(3, 8, F) for k in range(3)]
                for s in range(SB):
                    row = pl.ds(a * SB + s, 8, stride=0)
                    for k in range(3):
                        product = src[k][t, block, row][None] * held[k]
                        sums[s * 3 + k] = sums[s * 3 + k] + product.reshape(R, F)
            for i in range(3 * SB):
                hist[chunk + 1, i] = sums[i]
        cut = order_ref[N_CHUNK * CHUNK]
        for s in range(SB):
            early = [hist[cut, 3 * s + k] for k in range(3)]
            late = [sums[3 * s + k] - early[k] for k in range(3)]
            for group, (one, two, three) in enumerate((early, late)):
                cross[group, s, :, 0:F] = one + two
                cross[group, s, :, F : 2 * F] = three - one + two
        both = cross[...].reshape(G * SB * R, 2 * F)
        upper = both.astype(jnp.bfloat16)
        lower = (both - upper.astype(jnp.float32)).astype(jnp.bfloat16)
        wide = jnp.dot(upper, table_ref[...], preferred_element_type=jnp.float32)
        narrow = jnp.dot(lower, table_ref[:, 0:LAG], preferred_element_type=jnp.float32)
        lagged = (wide[:, :LAG] + wide[:, LAG:] + narrow).reshape(G, SB, R, LAG)
        for group in range(G):
            scale = scale_ref[group, 0:1]
            put = (pair % 2 * G + group) * PB
            for s in range(SB):
                rows = lagged[group, s] * scale
                for q in range(R // PB):
                    part[pair // 2, (block * SB + s) * 4 + q, put : put + PB] = rows[q * PB : (q + 1) * PB]

    lane = lax.broadcasted_iota(jnp.int32, (ROWS, LAG), 1)
    line = lax.broadcasted_iota(jnp.int32, (ROWS, LAG), 0)
    end = len(ROUNDS) - 1
    height = [ROWS] * end + [LAST]
    diagonal = [(lane == line + n * ROWS)[: height[n]] for n in range(end + 1)]

    def parcel(n, step):
        source, target = (coded_last, slots_last) if n == end else (coded.at[n], slots.at[n])
        return push(
            source.at[step - 1], target.at[step - 1], d_send.at[n, step - 1], d_recv.at[n, step - 1],
            {"day": lax.rem(day + step, N_DAY)},
        )

    def post(n):
        for first in range(0, N_DAY - 1, BATCH):
            steps = both_ways(N_DAY)[first : first + BATCH]
            for step in steps:
                rows = part[n, block_ref[lax.rem(day + step, N_DAY)], 0 : height[n]]
                largest = jnp.max(jnp.abs(rows), axis=1, keepdims=True)
                level = jnp.ceil(jnp.log2(jnp.maximum(largest, 1e-30)) * STEPS)
                values = rows * (jnp.exp2(level * (-1.0 / STEPS)) * PEAK)
                if n == end:
                    level, at = level[:PAIR], diagonal[n][:PAIR]
                else:
                    at = diagonal[n]
                mine_levels = jnp.sum(jnp.where(at, level, 0.0), axis=0, keepdims=True)
                if n:
                    mine_levels += levels[step - 1]
                if n < end:
                    levels[step - 1] = mine_levels
                    coded[n, step - 1] = jnp.round(values).astype(jnp.int32).astype(jnp.int16)
                else:
                    values = jnp.where(line[:LAST] == PAIR, mine_levels, values)
                    coded_last[step - 1] = jnp.round(values).astype(jnp.int32).astype(jnp.int16)
            for step in steps:
                parcel(n, step).start()

    def finish():
        totals = [part[n, block_ref[day], 0 : height[n]] for n in range(end + 1)]
        for first in range(0, N_DAY - 1, BATCH):
            steps = both_ways(N_DAY)[first : first + BATCH]
            for step in steps:
                for n in range(end + 1):
                    parcel(n, step).wait_recv()
            for step in steps:
                values = [slots[n, step - 1] for n in range(end)] + [slots_last[step - 1]]
                values = [v.astype(jnp.int32).astype(jnp.float32) for v in values]
                coding = values[end][PAIR : PAIR + 1]
                for n in range(end + 1):
                    level = jnp.sum(jnp.where(diagonal[n], coding, 0.0), axis=1, keepdims=True)
                    totals[n] += values[n] * (jnp.exp2(level * (1.0 / STEPS)) * (1.0 / PEAK))
        for pair in range(9):
            for group in range(G):
                row = (pair % 2 * G + group) * PB
                for r in range(PB):
                    out_ref[r, pair, group : group + 1, :] = totals[pair // 2][row + r : row + r + 1]

    def twice(pair):
        def body(block, carry):
            unit(pair, block)
            return carry

        lax.fori_loop(0, 2, body, 0)

    hand_over(0)
    take(0)
    hand_over(1)
    for pair in ROUNDS[0]:
        unit(pair, 0)
    take(1)
    for pair in ROUNDS[0]:
        unit(pair, 1)
    post(0)
    for n in range(1, end + 1):
        for pair in ROUNDS[n]:
            twice(pair)
        post(n)
    finish()
    for copy in started:
        copy.wait_send()

    def settle(j, carry):
        for n in range(end + 1):
            parcel(n, 1 + j).wait_send()
        return carry

    lax.fori_loop(0, N_DAY - 1, settle, 0)


def main(src_block, order, block_at, scale, spectra):
    pieces = spectra.reshape(N_STA, PIECE, 2, 3, R, F)
    half = N_STA // 2
    vmem = pl.BlockSpec(memory_space=pltpu.VMEM)
    smem = pl.BlockSpec(memory_space=pltpu.SMEM)
    dma = pltpu.SemaphoreType.DMA
    rec = pltpu.VMEM((SEG + 1, 3, R, F), jnp.float32)
    src = pltpu.VMEM((SEG + 1, 2, 3 * SB, F), jnp.float32)
    rows = pltpu.VMEM((N_STA, PIECE, 6 * SB, F), jnp.bfloat16)
    coded = pltpu.VMEM((len(ROUNDS) - 1, N_DAY - 1, ROWS, LAG), jnp.int16)
    last = pltpu.VMEM((N_DAY - 1, LAST, LAG), jnp.int16)
    return pl.pallas_call(
        main_kernel,
        out_shape=jax.ShapeDtypeStruct((PB, 9, G, LAG), jnp.float32),
        in_specs=[smem, smem, smem, vmem, vmem, pl.BlockSpec(memory_space=pl.ANY)],
        out_specs=vmem,
        scratch_shapes=[
            pltpu.VMEM(pieces.shape, jnp.bfloat16),
            rows, rows,
            pltpu.VMEM((N_STA, 2, PIECE, 6 * SB, F), jnp.bfloat16),
            rec, rec, rec, src, src, src,
            pltpu.VMEM((N_CHUNK + 1, 3 * SB, R, F), jnp.float32),
            pltpu.VMEM((G, SB, R, 2 * F), jnp.float32),
            pltpu.VMEM((len(ROUNDS), N_DAY, ROWS, LAG), jnp.float32),
            coded, coded, last, last,
            pltpu.VMEM((N_DAY - 1, 1, LAG), jnp.float32),
            dma((2,)),
            dma((N_STA - 1,)), dma((N_STA - 1,)),
            dma((2, half - 1)), dma((2, half - 1)),
            dma((2, half)), dma((2, half)),
            dma((len(ROUNDS), N_DAY - 1)), dma((len(ROUNDS), N_DAY - 1)),
        ],
        compiler_params=pltpu.CompilerParams(
            collective_id=0, has_side_effects=True, vmem_limit_bytes=VMEM_LIMIT
        ),
        name="main",
    )(src_block, order, block_at, scale, jnp.asarray(lag_tables()), pieces)


def local(spectra, src_block, group_of, owner):
    day = lax.axis_index("day").astype(jnp.int32).reshape(1)
    order, block_at, scale = plan(day, group_of, owner)
    return main(src_block, order, block_at, scale, spectra).transpose(0, 2, 1, 3)[None]


def solution(mesh):
    return jax.shard_map(
        local,
        mesh=mesh,
        in_specs=(P("day", None, None, "sta", None), P(), P(), P()),
        out_specs=P("day", "sta", None, None, None),
        check_vma=False,
    )
```
